32 devices in a mesh: row: 8 (over z, core), col: 4 (over y, x).
Axes of the slice: x: 2, y: 2, z: 4, core: 2. Of those that a mesh axis runs over, the one named last changes fastest.
Arguments:
- gram: bfloat16 [32768, 32768], P('row', 'col'), may hold values from -1 to 5, as said below
- start_basis: bfloat16 [32768, 256], P(('row', 'col')), may hold values from -12 to 12
- slab: float32 [32768, 4096], P('row', 'col'), may hold values from -6 to 6
Outputs:
- core_scaled: float32 [32768, 256], P(('row', 'col'))
- next_unfolding: float32 [4096, 256], P(('row', 'col'))
The draws below stay inside these ranges and needn't reach their ends.
Inputs may be any that keep to these rules, and one draw needn't show every extreme that they name: gram is symmetric: entry (i, j) equals entry (j, i).
All inputs are finite; a program needn't handle non-finite values.
Results may differ from the reference program's by a relative error of at most 0.003.
Values may be sent and summed in bfloat16 or wider, within the bound.
A program may use at most 192 MiB of HBM per device.

```python
import math
import jax
import jax.numpy as jnp
from jax import lax

N = 32768
P_SIZE = 256
NMODE = 16
REST = 256
W = 4096


def draw_gram(key, part):
    span = math.gcd(N, 512)
    blocks = N // span
    off_scale = 0.3 / math.sqrt(N)
    position = jnp.arange(N, dtype=jnp.float32) / N
    spread = 1.8
    factors = jnp.exp(jax.random.uniform(jax.random.fold_in(key, 12), (N,), minval=0.0, maxval=math.log(spread)))
    diagonal = 0.5 * jnp.exp(position * math.log(3.0)) * factors
    tile_key = jax.random.fold_in(key, 11)

    def one_tile(row_block, col_block):
        lesser = jnp.minimum(row_block, col_block)
        greater = jnp.maximum(row_block, col_block)
        sub_key = jax.random.fold_in(tile_key, lesser * blocks + greater)
        base = jnp.clip(jax.random.normal(sub_key, (span, span)), -6.0, 6.0)
        mirror = base.T
        tile = jnp.where(row_block < col_block, base, jnp.where(row_block > col_block, mirror, (base + mirror) * 0.70710678))
        segment = lax.dynamic_slice_in_dim(diagonal, row_block * span, span, 0)
        on_diag = jnp.where(row_block == col_block, 1.0, 0.0)
        return tile * off_scale + on_diag * jnp.diag(segment)

    def block_row(row_block):
        tiles = jax.vmap(lambda col_block: one_tile(row_block, col_block))(jnp.arange(blocks))
        return tiles.astype(jnp.bfloat16)
    stacked = lax.map(block_row, jnp.arange(blocks))
    return stacked.transpose(0, 2, 1, 3).reshape(N, N)


def draw_start_basis(key, part):
    scale_key, main_key = jax.random.split(jax.random.fold_in(key, 21), 2)
    scales = jnp.exp(jax.random.uniform(scale_key, (P_SIZE,), minval=math.log(0.3), maxval=math.log(3.0)))
    base = jnp.clip(jax.random.normal(main_key, (N, P_SIZE)), -6.0, 6.0)
    return jnp.clip(base * scales[None, :], -12.0, 12.0).astype(jnp.bfloat16)


def block_scale(rng, dims, cuts, least, high):
    loudness = 1.0
    for dim, shards_of in cuts:
        draws = jax.random.uniform(jax.random.fold_in(jax.random.fold_in(rng, 6), dim), (shards_of,), jnp.float32, least / len(cuts), high / len(cuts))
        loudness = loudness * jnp.repeat(jnp.exp(draws), dims[dim] // shards_of).reshape((-1,) + (1,) * (len(dims) - 1 - dim))
    return loudness


def noise(key, dims, scale, reach, cuts=(), held_as=jnp.bfloat16):
    values = jax.random.normal(key, dims, jnp.float32) * scale
    if len(cuts) > 0:
        values = block_scale(key, dims, cuts, -0.22, 0.18) * values
    return jnp.clip(values, min=-reach, max=reach).astype(held_as)


def setup_inputs(seed: int = 0) -> dict:
    seeds = jax.random.split(jax.random.key(seed), 4)
    return {
        "gram": draw_gram(jax.random.fold_in(seeds[3], 71), 0),
        "start_basis": draw_start_basis(jax.random.fold_in(seeds[3], 71), 0),
        "slab": noise(seeds[2], (N, W), 1.0, 6.0, ((0, 8), (1, 4)), jnp.float32),
    }


def gram_times(gram, source):
    span = math.gcd(N, 4096)
    source_wide = source.astype(jnp.float32)

    def one_block(rows_block):
        return jnp.dot(rows_block.astype(jnp.float32), source_wide, precision=lax.Precision.HIGHEST)
    pieces = lax.map(one_block, gram.reshape(N // span, span, N))
    return pieces.reshape(N, source.shape[1])

def reference(gram, start_basis, slab):
    first_image = gram_times(gram, start_basis).astype(jnp.bfloat16)
    second_image = gram_times(gram, first_image)
    small_gram = jnp.dot(second_image.T, second_image, precision=lax.Precision.HIGHEST)
    factor = jnp.linalg.cholesky(small_gram)
    basis_cols = jax.scipy.linalg.solve_triangular(factor, second_image.T, lower=True).T
    core_scaled = basis_cols * math.sqrt(N)
    projection = jnp.dot(basis_cols.T, slab, precision=lax.Precision.HIGHEST)
    next_unfolding = projection.reshape(P_SIZE * NMODE, REST)
    return (core_scaled, next_unfolding)
```

```python
import math

import jax
import jax.numpy as jnp
from jax import lax
from jax.experimental import pallas as pl
from jax.experimental.layout import Layout, with_layout_constraint
from jax.experimental.pallas import tpu as pltpu
from jax.sharding import PartitionSpec as P

HIGHEST = lax.Precision.HIGHEST
CONTRACT_ROWS = (((0,), (0,)), ((), ()))
CHUNKS = 2


def flip(value, axis, mask):
    size = lax.axis_size(axis)
    return lax.ppermute(value, axis, [(i, i ^ mask) for i in range(size)])


def gather_flips(block, axis):
    size, me = lax.axis_size(axis), lax.axis_index(axis)
    arrived = [block] + [flip(block, axis, mask) for mask in range(1, size)]
    stacked = jnp.zeros((size,) + block.shape, block.dtype)
    for mask, piece in enumerate(arrived):
        stacked = lax.dynamic_update_slice_in_dim(stacked, piece[None], me ^ mask, 0)
    return stacked.reshape((size * block.shape[0],) + block.shape[1:])


def scatter_sum_flips(parts, axis, wire):
    size, me = lax.axis_size(axis), lax.axis_index(axis)
    share = parts.shape[0] // size
    take = lambda owner: lax.dynamic_slice_in_dim(parts, owner * share, share, 0)
    total = take(me)
    for mask in range(1, size):
        total = total + flip(take(me ^ mask).astype(wire), axis, mask).astype(jnp.float32)
    return total


def sum_rows(value, beside):
    size, me = lax.axis_size("row"), lax.axis_index("row")
    core = me % 2
    half = value.shape[0] // 2
    take = lambda index: lax.dynamic_slice_in_dim(value, index * half, half, 0)
    pair = take(core) + flip(take(1 - core), "row", 1)
    arrived = [flip(pair, "row", mask) for mask in range(2, size, 2)]
    arrived, beside = lax.optimization_barrier((arrived, beside))
    total = pair
    for piece in arrived:
        total = total + piece
    back = flip(total, "row", 1)
    low = jnp.where(core == 0, total, back)
    high = jnp.where(core == 0, back, total)
    return jnp.concatenate([low, high], axis=0), beside


def dot32(a, b, dims=(((1,), (0,)), ((), ()))):
    return lax.dot_general(a, b, dims, precision=HIGHEST, preferred_element_type=jnp.float32)


ALONG = (((1,), (1,)), ((), ()))


def invert_block(work):
    n = work.shape[0]
    lane = lax.broadcasted_iota(jnp.int32, (1, n), 1)
    down = lax.broadcasted_iota(jnp.int32, (n, 1), 0)

    def step(j, pivots):
        values = work[...]
        row = work[pl.ds(j, 1), :]
        here = lane == j
        column = jnp.sum(jnp.where(here, values, 0.0), axis=1, keepdims=True)
        pivot = jnp.sum(jnp.where(here, row, 0.0), axis=1, keepdims=True)
        multiple = jnp.where(down > j, column / pivot, 0.0)
        kept = jnp.where(here & (down > j), 0.0, values)
        work[...] = kept - multiple * jnp.where(here, 1.0, row)
        return jnp.where(down == j, pivot, pivots)

    pivots = lax.fori_loop(0, n, step, jnp.ones((n, 1), jnp.float32))
    across = lax.broadcasted_iota(jnp.int32, (n, n), 1)
    unit = jnp.where(across < down, work[...], jnp.where(across == down, 1.0, 0.0))
    return unit * lax.rsqrt(pivots)


def inverse_kernel(gram_ref, out_ref, work):
    half = work.shape[0]
    work[...] = gram_ref[:half, :half]
    inv11 = invert_block(work)
    a21 = gram_ref[half:, :half]
    l21 = dot32(a21, inv11, ALONG)
    work[...] = gram_ref[half:, half:] - dot32(l21, l21, ALONG)
    inv22 = invert_block(work)
    out_ref[:half, :half] = inv11
    out_ref[:half, half:] = jnp.zeros((half, half), jnp.float32)
    out_ref[half:, :half] = -dot32(inv22, dot32(l21, inv11))
    out_ref[half:, half:] = inv22


def inverse_factor(small_gram):
    half = small_gram.shape[0] // 2
    return pl.pallas_call(
        inverse_kernel,
        out_shape=jax.ShapeDtypeStruct(small_gram.shape, jnp.float32),
        scratch_shapes=[pltpu.VMEM((half, half), jnp.float32)],
        name="inverse_factor",
    )(small_gram)


def gram_kernel(y_ref, out_ref):
    @pl.when(pl.program_id(0) == 0)
    def _():
        out_ref[...] = jnp.zeros_like(out_ref)

    y = y_ref[...]
    out_ref[...] += lax.dot_general(y, y, CONTRACT_ROWS, preferred_element_type=jnp.float32)


def block_gram(y):
    tile = math.gcd(y.shape[0], 1024)
    size = y.shape[1]
    return pl.pallas_call(
        gram_kernel,
        grid=(y.shape[0] // tile,),
        in_specs=[pl.BlockSpec((tile, size), lambda i: (i, 0))],
        out_specs=pl.BlockSpec((size, size), lambda i: (0, 0)),
        out_shape=jax.ShapeDtypeStruct((size, size), jnp.float32),
        name="block_gram",
        cost_estimate=pl.CostEstimate(
            flops=2 * y.shape[0] * size * size, bytes_accessed=2 * y.size, transcendentals=0
        ),
    )(y)


def cross_kernel(slab_ref, y_ref, out_ref):
    @pl.when(pl.program_id(0) == 0)
    def _():
        out_ref[...] = jnp.zeros_like(out_ref)

    y = y_ref[...]
    slab = slab_ref[...]
    high = slab.astype(jnp.bfloat16)
    low = (slab - high.astype(jnp.float32)).astype(jnp.bfloat16)
    term = lambda a: lax.dot_general(a, y, CONTRACT_ROWS, preferred_element_type=jnp.float32)
    out_ref[...] += term(high) + term(low)


def cross_product(slab, y):
    tile = math.gcd(y.shape[0], 512)
    wide, size = slab.shape[1], y.shape[1]
    return pl.pallas_call(
        cross_kernel,
        grid=(y.shape[0] // tile,),
        in_specs=[
            pl.BlockSpec((tile, wide), lambda i: (i, 0)),
            pl.BlockSpec((tile, size), lambda i: (i, 0)),
        ],
        out_specs=pl.BlockSpec((wide, size), lambda i: (0, 0)),
        out_shape=jax.ShapeDtypeStruct((wide, size), jnp.float32),
        name="cross_product",
        cost_estimate=pl.CostEstimate(
            flops=4 * slab.size * size, bytes_accessed=4 * slab.size, transcendentals=0
        ),
    )(slab, y)


def body(gram, start_basis, slab, order, modes):
    rows, cols = lax.axis_size("row"), lax.axis_size("col")
    own_rows = gather_flips(start_basis, "col")
    span = gram.shape[1] // CHUNKS
    partial = None
    for chunk in range(CHUNKS):
        block = gram[:, chunk * span : (chunk + 1) * span]
        first = lax.psum_scatter(
            lax.dot_general(block, own_rows, CONTRACT_ROWS, preferred_element_type=jnp.float32),
            "row",
            scatter_dimension=0,
            tiled=True,
        ).astype(jnp.bfloat16)
        image = lax.all_gather(first, "row", axis=0, tiled=True)
        term = jnp.dot(block, image, preferred_element_type=jnp.float32)
        partial = term if partial is None else partial + term
    partial = with_layout_constraint(partial, Layout((0, 1)))
    second = scatter_sum_flips(partial, "col", jnp.bfloat16)
    block_second = gather_flips(second.astype(jnp.bfloat16), "col")
    small_gram, crossed = sum_rows(block_gram(block_second), cross_product(slab, block_second))
    crossed = lax.psum_scatter(crossed, "row", scatter_dimension=0, tiled=True)
    inverse = inverse_factor(small_gram)
    proj = dot32(inverse, crossed, ALONG)
    core_out = dot32(second, inverse, ALONG) * math.sqrt(order)
    count = rows * cols
    share = proj.shape[0] // count
    moved = lax.all_to_all(
        proj.reshape(count, share, proj.shape[1]), ("row", "col"), split_axis=0, concat_axis=0, tiled=True
    )
    moved = moved.reshape(rows, cols, share, proj.shape[1]).transpose(2, 1, 0, 3)
    return core_out, moved.reshape(share * modes, -1)


NMODE = 16


def solution(mesh):
    def whole(gram, start_basis, slab):
        order = gram.shape[0]
        inner = lambda g, s, w: body(g, s, w, order, NMODE)
        in_specs = (P("row", "col"), P(("row", "col"), None), P("row", "col"))
        out_specs = (P(("row", "col"), None), P(("row", "col"), None))
        return jax.shard_map(
            inner, mesh=mesh, in_specs=in_specs, out_specs=out_specs, check_vma=False
        )(gram, start_basis, slab)

    return whole
```
